512 devices in a mesh: tensor: 64 (over x, y, core), replica: 8 (over z).
Axes of the slice: x: 4, y: 8, z: 8, core: 2. Of those that a mesh axis runs over, the one named last changes fastest.
Arguments:
- amplitudes: bfloat16 [1024, 64, 128], P('tensor'), may hold values from -6 to 6
- block_slot: int32 [1024], replicated, may hold values from 0 to 1023, each once
- integrals: bfloat16 [1024, 64, 64, 64], P('tensor', 'replica'), may hold values from -0.09375 to 0.09375
- tile_cols: int32 [1024, 64], P('tensor'), may hold values from 0 to 1023, as said below
- irreps: int32 [1024], replicated, may hold values from 0 to 7, as said below
Outputs:
- ladder: float32 [1024, 64, 128], P('tensor', None, 'replica')
The draws below stay inside these ranges and needn't reach their ends.
Inputs may be any that keep to these rules, and one draw needn't show every extreme that they name: `block_slot`: each block has one slot and each slot one block. `tile_cols`: the tiles of a row that name blocks of the row's own irrep name distinct blocks; other tiles may name any block of another irrep. `irreps`: each irrep labels exactly 128 blocks.
All inputs are finite; a program needn't handle non-finite values.
Results may differ from the reference program's by a relative error of at most 0.0003.
Values may be sent and summed in bfloat16 or wider, within the bound.
No kernel may reach another device: no remote copies, remote signals or barrier semaphores. Data moves between devices by JAX's collectives and lax.ppermute only.
A program may use at most 128 MiB of HBM per device.

```python
import jax
import jax.numpy as jnp
from jax import lax

TILE = 64
OCCP = 128
NIRR = 8
NBLK = 1024
NZ_ROW = 64


def symmetry_labels(key):
    shuffled = jax.random.permutation(jax.random.fold_in(key, 11), NBLK).astype(jnp.int32)
    labels = (shuffled % NIRR).astype(jnp.int32)
    members = jnp.zeros((NBLK,), jnp.int32).at[shuffled].set(jnp.arange(NBLK, dtype=jnp.int32))
    return (labels, members)


def draw_irreps(key, part):
    labels, members = symmetry_labels(key)
    return labels


def draw_tile_cols(key, part):
    labels, members = symmetry_labels(key)
    per_irrep = NBLK // NIRR
    scores = jax.random.randint(jax.random.fold_in(key, 21), (NBLK, per_irrep), 0, 1 << 20).astype(jnp.int32)
    scores = scores * per_irrep + jnp.arange(per_irrep, dtype=jnp.int32)[None, :]
    ranks = jnp.argsort(scores, axis=1)[:, :NZ_ROW].astype(jnp.int32)
    own_cols = members[labels[:, None] + NIRR * ranks]
    flipped = jax.random.randint(jax.random.fold_in(key, 31), (NBLK, NZ_ROW), 0, 8) == 0
    offset = jax.random.randint(jax.random.fold_in(key, 41), (NBLK, NZ_ROW), 1, NIRR).astype(jnp.int32)
    other_irrep = (labels[:, None] + offset) % NIRR
    other_rank = jax.random.randint(jax.random.fold_in(key, 51), (NBLK, NZ_ROW), 0, per_irrep).astype(jnp.int32)
    other_cols = members[other_irrep + NIRR * other_rank]
    return jnp.where(flipped, other_cols, own_cols).astype(jnp.int32)


def level_of(rng, dims, pieces, low, largest):
    level = 1.0
    for dim, shards_of in pieces:
        draws = jax.random.uniform(jax.random.fold_in(jax.random.fold_in(rng, 6), dim), (shards_of,), jnp.float32, low / len(pieces), largest / len(pieces))
        level = level * jnp.repeat(jnp.exp(draws), dims[dim] // shards_of).reshape((-1,) + (1,) * (len(dims) - 1 - dim))
    return level


def bell_draw(own_key, shape, spread, reach, split=(), held_as=jnp.bfloat16):
    result = jax.random.normal(own_key, shape, jnp.float32) * spread
    if len(split) > 0:
        result = level_of(own_key, shape, split, -0.22, 0.18) * result
    return jnp.clip(result, min=-reach, max=reach).astype(held_as)


def setup_inputs(seed: int = 0) -> dict:
    keys = jax.random.split(jax.random.key(seed), 6)
    amplitudes = bell_draw(keys[0], (NBLK, TILE, OCCP), 1.0, 6.0, ((0, 64),))
    block_slot = jax.random.permutation(keys[1], NBLK).astype(jnp.int32)
    integrals = bell_draw(keys[2], (NBLK, NZ_ROW, TILE, TILE), (TILE * NZ_ROW) ** -0.5, 0.09375, ((0, 64), (1, 8)))
    tile_cols = draw_tile_cols(jax.random.fold_in(keys[5], 71), 0)
    irreps = draw_irreps(jax.random.fold_in(keys[5], 71), 0)
    return {"amplitudes": amplitudes, "block_slot": block_slot, "integrals": integrals, "tile_cols": tile_cols, "irreps": irreps}


def reference(amplitudes, block_slot, integrals, tile_cols, irreps):
    natural = amplitudes[block_slot]

    def one_row(index):
        cols = tile_cols[index]
        allowed = (irreps[cols] == irreps[index]).astype(jnp.bfloat16)
        tiles = integrals[index] * allowed[:, None, None]
        picked = natural[cols]
        return jnp.einsum("nxy,nyp->xp", tiles.astype(jnp.float32), picked.astype(jnp.float32), precision=lax.Precision.HIGHEST)

    return lax.map(one_row, jnp.arange(NBLK, dtype=jnp.int32))
```

```python
import jax
import jax.numpy as jnp
from jax import lax
from jax.experimental import pallas as pl
from jax.experimental.pallas import tpu as pltpu
from jax.sharding import Mesh, PartitionSpec as P

NX, NY, NC, NZ = 4, 8, 2, 8
BLK = 1024
ROWS = 16
PAIRS = ROWS // 2
TILE = 64
SUB = TILE // NZ
PER_Z = 8
OCC = 128
CONTR = NZ * PER_Z * SUB

bf16 = jnp.bfloat16
f32 = jnp.float32


def split_tiles(tiles_ref, out_ref):
    eye = (
        lax.broadcasted_iota(jnp.int32, (TILE, TILE), 0)
        == lax.broadcasted_iota(jnp.int32, (TILE, TILE), 1)
    ).astype(bf16)

    def step(pair, carry):
        for n in range(PER_Z):
            both = jnp.concatenate(
                [tiles_ref[2 * pair, n], tiles_ref[2 * pair + 1, n]], axis=0
            )
            turned = lax.dot_general(
                eye, both, (((1,), (1,)), ((), ())), preferred_element_type=f32
            ).astype(bf16)
            for z in range(NZ):
                out_ref[z, pair, n * SUB : (n + 1) * SUB, :] = turned[
                    z * SUB : (z + 1) * SUB, :
                ]
        return carry

    lax.fori_loop(0, PAIRS, step, 0)


def contract(where_ref, own_hbm, other_hbm, tiles_ref, out_ref, amp, picked, sem):
    half = BLK // NC
    first = pltpu.make_async_copy(own_hbm, amp.at[pl.ds(0, half)], sem.at[0])
    second = pltpu.make_async_copy(other_hbm, amp.at[pl.ds(half, half)], sem.at[1])
    first.start()
    second.start()
    amp[BLK] = jnp.zeros((SUB, OCC), bf16)
    low = lax.broadcasted_iota(jnp.int32, (OCC, OCC), 1) < TILE
    first.wait()
    second.wait()

    def step(pair, carry):
        for parity in range(2):
            for n in range(NZ * PER_Z):
                at = where_ref[2 * pair + parity, n]
                picked[n * SUB : (n + 1) * SUB, parity * OCC : (parity + 1) * OCC] = (
                    amp[at]
                )
        tiles = tiles_ref[:, pair].reshape(CONTR, OCC)
        both = lax.dot_general(
            picked[...], tiles, (((0,), (0,)), ((), ())), preferred_element_type=f32
        )
        out_ref[:, pair] = jnp.where(low, both[:OCC], both[OCC:]).reshape(
            NZ, OCC // NZ, OCC
        )
        return carry

    lax.fori_loop(0, PAIRS, step, 0)


def add_up(parts_ref, out_ref):
    total = parts_ref[0]
    for z in range(1, NZ):
        total = total + parts_ref[z]
    for pair in range(PAIRS):
        out_ref[2 * pair] = total[pair, :, :TILE]
        out_ref[2 * pair + 1] = total[pair, :, TILE:]


def in_vmem(n):
    return [pl.BlockSpec(memory_space=pltpu.VMEM)] * n


def local(amplitudes, block_slot, integrals, tile_cols, irreps):
    x, y = lax.axis_index("x"), lax.axis_index("y")
    core, z = lax.axis_index("core"), lax.axis_index("z")

    part = lax.dynamic_slice_in_dim(amplitudes, z * SUB, SUB, 1)
    along_y = lax.all_to_all(
        jnp.broadcast_to(part, (NY, ROWS, SUB, OCC)), "y", 0, 0, tiled=False
    )
    along_x = lax.all_to_all(
        jnp.broadcast_to(along_y, (NX, NY, ROWS, SUB, OCC)), "x", 0, 0, tiled=False
    )
    own = along_x.reshape(BLK // NC, SUB, OCC)
    other = lax.ppermute(own, "core", [(0, 1), (1, 0)])

    split = pl.pallas_call(
        split_tiles,
        out_shape=jax.ShapeDtypeStruct((NZ, PAIRS, PER_Z * SUB, OCC), bf16),
        in_specs=in_vmem(1),
        out_specs=in_vmem(1)[0],
        cost_estimate=pl.CostEstimate(
            flops=1 << 28, bytes_accessed=3 << 20, transcendentals=0
        ),
        name="split_tiles",
    )(integrals)
    tiles = lax.all_to_all(split, "z", 0, 0, tiled=False)

    first_row = ((x * NY + y) * NC + core) * ROWS
    row_irrep = lax.dynamic_slice_in_dim(irreps, first_row, ROWS, 0)
    slot = block_slot[tile_cols]
    allowed = irreps[tile_cols] == row_irrep[:, None]
    holder = slot // ROWS
    place = (holder // NC) * ROWS + slot % ROWS
    place = place + jnp.where(holder % NC == core, 0, BLK // NC)
    where = jnp.where(allowed, place, BLK)

    sums = pl.pallas_call(
        contract,
        out_shape=jax.ShapeDtypeStruct((NZ, PAIRS, OCC // NZ, OCC), f32),
        in_specs=[
            pl.BlockSpec(memory_space=pltpu.SMEM),
            pl.BlockSpec(memory_space=pl.ANY),
            pl.BlockSpec(memory_space=pl.ANY),
            pl.BlockSpec(memory_space=pltpu.VMEM),
        ],
        out_specs=in_vmem(1)[0],
        scratch_shapes=[
            pltpu.VMEM((BLK + 8, SUB, OCC), bf16),
            pltpu.VMEM((CONTR, 2 * OCC), bf16),
            pltpu.SemaphoreType.DMA((2,)),
        ],
        cost_estimate=pl.CostEstimate(
            flops=1 << 28, bytes_accessed=4 << 20, transcendentals=0
        ),
        name="contract",
    )(where, own, other, tiles)
    parts = lax.all_to_all(sums, "z", 0, 0, tiled=False)

    total = pl.pallas_call(
        add_up,
        out_shape=jax.ShapeDtypeStruct((ROWS, OCC // NZ, TILE), f32),
        in_specs=in_vmem(1),
        out_specs=in_vmem(1)[0],
        name="add_up",
    )(parts)
    return jnp.swapaxes(total, 1, 2)


def solution(mesh):
    fine = Mesh(mesh.devices.reshape(NX, NY, NC, NZ), ("x", "y", "core", "z"))
    tensor = ("x", "y", "core")
    in_specs = (
        P(tensor, None, None),
        P(),
        P(tensor, "z", None, None),
        P(tensor, None),
        P(),
    )
    return jax.shard_map(
        local, mesh=fine, in_specs=in_specs, out_specs=P(tensor, None, "z"), check_vma=False
    )
```

```python
import jax
import jax.numpy as jnp
from jax import lax
from jax.experimental import pallas as pl
from jax.experimental.pallas import tpu as pltpu
from jax.sharding import Mesh, PartitionSpec as P


NX, NY, NC, NZ = 4, 8, 2, 8
BLK = 1024
ROWS = 16
PAIRS = ROWS // 2
TILE = 64
SUB = TILE // NZ
PER_Z = 8
OCC = 128
VMEM = 16 << 20
CONTR = NZ * PER_Z * SUB

bf16 = jnp.bfloat16
f32 = jnp.float32


def split_tiles(tiles_ref, out_ref):
    eye = (
        lax.broadcasted_iota(jnp.int32, (TILE, TILE), 0)
        == lax.broadcasted_iota(jnp.int32, (TILE, TILE), 1)
    ).astype(bf16)

    def step(pair, carry):
        for n in range(PER_Z):
            both = jnp.concatenate(
                [tiles_ref[2 * pair, n], tiles_ref[2 * pair + 1, n]], axis=0
            )
            turned = lax.dot_general(
                eye, both, (((1,), (1,)), ((), ())), preferred_element_type=f32
            ).astype(bf16)
            for z in range(NZ):
                out_ref[z, pair, n * SUB : (n + 1) * SUB, :] = turned[
                    z * SUB : (z + 1) * SUB, :
                ]
        return carry

    lax.fori_loop(0, PAIRS, step, 0)


def pick(where_ref, *refs):
    pieces, out_ref, amp, sem = refs[:-3], *refs[-3:]
    size = BLK // len(pieces)
    copies = [
        pltpu.make_async_copy(piece, amp.at[pl.ds(k * size, size)], sem.at[k])
        for k, piece in enumerate(pieces)
    ]
    for copy in copies:
        copy.start()
    amp[BLK] = jnp.zeros((SUB, OCC), bf16)
    for copy in copies:
        copy.wait()

    def step(pair, carry):
        for parity in range(2):
            for n in range(NZ * PER_Z):
                at = where_ref[2 * pair + parity, n]
                out_ref[
                    pair, n * SUB : (n + 1) * SUB, parity * OCC : (parity + 1) * OCC
                ] = amp[at]
        return carry

    lax.fori_loop(0, PAIRS, step, 0)


def contract(picked_ref, tiles_ref, out_ref):
    low = lax.broadcasted_iota(jnp.int32, (OCC, OCC), 1) < TILE
    for pair in range(PAIRS):
        tiles = tiles_ref[:, pair].reshape(CONTR, OCC)
        both = lax.dot_general(
            picked_ref[pair], tiles, (((0,), (0,)), ((), ())), preferred_element_type=f32
        )
        out_ref[:, pair] = jnp.where(low, both[:OCC], both[OCC:]).reshape(
            NZ, OCC // NZ, OCC
        )


def add_up(parts_ref, out_ref):
    total = parts_ref[0]
    for z in range(1, NZ):
        total = total + parts_ref[z]
    for pair in range(PAIRS):
        out_ref[2 * pair] = total[pair, :, :TILE]
        out_ref[2 * pair + 1] = total[pair, :, TILE:]


def in_vmem(n):
    return [pl.BlockSpec(memory_space=pltpu.VMEM)] * n


def cost(mib):
    return pl.CostEstimate(
        flops=1 << 28, bytes_accessed=mib << 20, transcendentals=0
    )


def local(amplitudes, block_slot, integrals, tile_cols, irreps):
    x, y = lax.axis_index("x"), lax.axis_index("y")
    core, z = lax.axis_index("core"), lax.axis_index("z")

    part = lax.dynamic_slice_in_dim(amplitudes, z * SUB, SUB, 1)
    to_y = jnp.broadcast_to(part, (NY, ROWS, SUB, OCC))
    along_y = lax.all_to_all(to_y, "y", 0, 0, tiled=False)
    own = [along_y.reshape(NY * ROWS, SUB, OCC)]
    for k in (1, 2, 3):
        shift = [((i + k) % NX, i) for i in range(NX)]
        own.append(lax.ppermute(own[0], "x", shift))
    other = []
    for piece in own:
        other.append(lax.ppermute(piece, "core", [(0, 1), (1, 0)]))

    split = pl.pallas_call(
        split_tiles,
        out_shape=jax.ShapeDtypeStruct((NZ, PAIRS, PER_Z * SUB, OCC), bf16),
        in_specs=in_vmem(1),
        out_specs=in_vmem(1)[0],
        compiler_params=pltpu.CompilerParams(vmem_limit_bytes=VMEM),
        cost_estimate=cost(3),
        name="split_tiles",
    )(integrals)
    tiles = lax.all_to_all(split, "z", 0, 0, tiled=False)

    table = block_slot * 8 + irreps
    first_row = ((x * NY + y) * NC + core) * ROWS
    row_irrep = lax.dynamic_slice_in_dim(irreps, first_row, ROWS, 0)
    found = table[tile_cols]
    slot, labels = found // 8, found % 8
    allowed = labels == row_irrep[:, None]
    holder = slot // ROWS
    holder_x, holder_y = holder // (NY * NC), (holder // NC) % NY
    place = ((holder_x - x) % NX) * NY + holder_y + (holder + core) % NC * (NX * NY)
    where = jnp.where(allowed, place * ROWS + slot % ROWS, BLK)

    picked = pl.pallas_call(
        pick,
        out_shape=jax.ShapeDtypeStruct((PAIRS, CONTR, 2 * OCC), bf16),
        in_specs=[pl.BlockSpec(memory_space=pltpu.SMEM)]
        + [pl.BlockSpec(memory_space=pl.ANY)] * (NX * NC),
        out_specs=in_vmem(1)[0],
        scratch_shapes=[
            pltpu.VMEM((BLK + 8, SUB, OCC), bf16),
            pltpu.SemaphoreType.DMA((NX * NC,)),
        ],
        compiler_params=pltpu.CompilerParams(vmem_limit_bytes=VMEM),
        cost_estimate=cost(6),
        name="pick",
    )(where, *own, *other)
    sums = pl.pallas_call(
        contract,
        out_shape=jax.ShapeDtypeStruct((NZ, PAIRS, OCC // NZ, OCC), f32),
        in_specs=in_vmem(2),
        out_specs=in_vmem(1)[0],
        compiler_params=pltpu.CompilerParams(vmem_limit_bytes=VMEM),
        cost_estimate=cost(4),
        name="contract",
    )(picked, tiles)
    parts = lax.all_to_all(sums, "z", 0, 0, tiled=False)

    total = pl.pallas_call(
        add_up,
        out_shape=jax.ShapeDtypeStruct((ROWS, OCC // NZ, TILE), f32),
        in_specs=in_vmem(1),
        out_specs=in_vmem(1)[0],
        compiler_params=pltpu.CompilerParams(vmem_limit_bytes=VMEM),
        cost_estimate=cost(1),
        name="add_up",
    )(parts)
    return jnp.swapaxes(total, 1, 2)


def solution(mesh):
    fine = Mesh(mesh.devices.reshape(NX, NY, NC, NZ), ("x", "y", "core", "z"))
    tensor = ("x", "y", "core")
    in_specs = (
        P(tensor, None, None),
        P(),
        P(tensor, "z", None, None),
        P(tensor, None),
        P(),
    )

    return jax.shard_map(
        local,
        mesh=fine,
        in_specs=in_specs,
        out_specs=P(tensor, None, "z"),
        check_vma=False,
    )
```

```python
import jax
import jax.numpy as jnp
from jax import lax
from jax.experimental import pallas as pl
from jax.experimental.pallas import tpu as pltpu
from jax.sharding import Mesh, PartitionSpec as P


NX, NY, NC, NZ = 4, 8, 2, 8
BLK = 1024
ROWS = 16
PAIRS = ROWS // 2
TILE = 64
NIRR = 8
SUB = TILE // NZ
PER_Z = 8
OCC = 128
VMEM = 16 << 20
CONTR = NZ * PER_Z * SUB

bf16 = jnp.bfloat16
f32 = jnp.float32


def split_tiles(tiles_ref, out_ref):
    eye = (
        lax.broadcasted_iota(jnp.int32, (TILE, TILE), 0)
        == lax.broadcasted_iota(jnp.int32, (TILE, TILE), 1)
    ).astype(bf16)

    def step(pair, carry):
        for n in range(PER_Z):
            both = jnp.concatenate(
                [tiles_ref[2 * pair, n], tiles_ref[2 * pair + 1, n]], axis=0
            )
            turned = lax.dot_general(
                eye, both, (((1,), (1,)), ((), ())), preferred_element_type=f32
            ).astype(bf16)
            for z in range(NZ):
                out_ref[z, pair, n * SUB : (n + 1) * SUB, :] = turned[
                    z * SUB : (z + 1) * SUB, :
                ]
        return carry

    lax.fori_loop(0, PAIRS, step, 0)


def find(table_ref, row_irrep_ref, cols_ref, out_ref):
    def step(row, carry):
        irrep = row_irrep_ref[row]
        for n in range(NZ * PER_Z):
            entry = table_ref[cols_ref[row, n]]
            out_ref[row, n] = jnp.where(
                jnp.bitwise_and(entry, NIRR - 1) == irrep,
                lax.shift_right_logical(entry, 3),
                BLK,
            )
        return carry

    lax.fori_loop(0, ROWS, step, 0)


def pick(where_ref, *refs):
    pieces, out_ref, amp, sem = refs[:-3], *refs[-3:]
    size = BLK // len(pieces)
    copies = [
        pltpu.make_async_copy(piece, amp.at[pl.ds(k * size, size)], sem.at[k])
        for k, piece in enumerate(pieces)
    ]
    for copy in copies:
        copy.start()
    amp[BLK] = jnp.zeros((SUB, OCC), bf16)
    for copy in copies:
        copy.wait()

    def step(pair, carry):
        for parity in range(2):
            for n in range(NZ * PER_Z):
                at = where_ref[2 * pair + parity, n]
                out_ref[
                    pair, n * SUB : (n + 1) * SUB, parity * OCC : (parity + 1) * OCC
                ] = amp[at]
        return carry

    lax.fori_loop(0, PAIRS, step, 0)


def contract(picked_ref, tiles_ref, out_ref):
    low = lax.broadcasted_iota(jnp.int32, (OCC, OCC), 1) < TILE
    for pair in range(PAIRS):
        tiles = tiles_ref[:, pair].reshape(CONTR, OCC)
        both = lax.dot_general(
            picked_ref[pair], tiles, (((0,), (0,)), ((), ())), preferred_element_type=f32
        )
        out_ref[:, pair] = jnp.where(low, both[:OCC], both[OCC:]).reshape(
            NZ, OCC // NZ, OCC
        )


def add_up(parts_ref, out_ref):
    total = parts_ref[0]
    for z in range(1, NZ):
        total = total + parts_ref[z]
    for pair in range(PAIRS):
        out_ref[2 * pair] = total[pair, :, :TILE]
        out_ref[2 * pair + 1] = total[pair, :, TILE:]


def in_vmem(n):
    return [pl.BlockSpec(memory_space=pltpu.VMEM)] * n


def cost(mib):
    return pl.CostEstimate(
        flops=1 << 28, bytes_accessed=mib << 20, transcendentals=0
    )


def local(amplitudes, block_slot, integrals, tile_cols, irreps):
    x, y = lax.axis_index("x"), lax.axis_index("y")
    core, z = lax.axis_index("core"), lax.axis_index("z")

    part = lax.dynamic_slice_in_dim(amplitudes, z * SUB, SUB, 1)
    along_y = lax.all_gather(part, "y", axis=0, tiled=True)
    pieces = [along_y]
    for k in (1, 2, 3):
        shift = [((i + k) % NX, i) for i in range(NX)]
        pieces.append(lax.ppermute(along_y, "x", shift))
    own = jnp.concatenate(pieces, axis=0)
    other = lax.ppermute(own, "core", [(0, 1), (1, 0)])

    split = pl.pallas_call(
        split_tiles,
        out_shape=jax.ShapeDtypeStruct((NZ, PAIRS, PER_Z * SUB, OCC), bf16),
        in_specs=in_vmem(1),
        out_specs=in_vmem(1)[0],
        compiler_params=pltpu.CompilerParams(vmem_limit_bytes=VMEM),
        cost_estimate=cost(3),
        name="split_tiles",
    )(integrals)
    tiles = lax.all_to_all(split, "z", 0, 0, tiled=False)

    holder = block_slot // ROWS
    holder_x, holder_y = holder // (NY * NC), (holder // NC) % NY
    place = ((holder_x - x) % NX) * NY + holder_y + (holder + core) % NC * (NX * NY)
    table = (place * ROWS + block_slot % ROWS) * NIRR + irreps
    first_row = ((x * NY + y) * NC + core) * ROWS
    row_irrep = lax.dynamic_slice_in_dim(irreps, first_row, ROWS, 0)
    where = pl.pallas_call(
        find,
        out_shape=jax.ShapeDtypeStruct((ROWS, NZ * PER_Z), jnp.int32),
        in_specs=[pl.BlockSpec(memory_space=pltpu.SMEM)] * 3,
        out_specs=pl.BlockSpec(memory_space=pltpu.SMEM),
        compiler_params=pltpu.CompilerParams(vmem_limit_bytes=VMEM),
        cost_estimate=cost(1),
        name="find",
    )(table, row_irrep, tile_cols)

    picked = pl.pallas_call(
        pick,
        out_shape=jax.ShapeDtypeStruct((PAIRS, CONTR, 2 * OCC), bf16),
        in_specs=[pl.BlockSpec(memory_space=pltpu.SMEM)]
        + [pl.BlockSpec(memory_space=pl.ANY)] * NC,
        out_specs=in_vmem(1)[0],
        scratch_shapes=[
            pltpu.VMEM((BLK + 8, SUB, OCC), bf16),
            pltpu.SemaphoreType.DMA((NC,)),
        ],
        compiler_params=pltpu.CompilerParams(vmem_limit_bytes=VMEM),
        cost_estimate=cost(6),
        name="pick",
    )(where, own, other)
    sums = pl.pallas_call(
        contract,
        out_shape=jax.ShapeDtypeStruct((NZ, PAIRS, OCC // NZ, OCC), f32),
        in_specs=in_vmem(2),
        out_specs=in_vmem(1)[0],
        compiler_params=pltpu.CompilerParams(vmem_limit_bytes=VMEM),
        cost_estimate=cost(4),
        name="contract",
    )(picked, tiles)
    parts = lax.all_to_all(sums, "z", 0, 0, tiled=False)

    total = pl.pallas_call(
        add_up,
        out_shape=jax.ShapeDtypeStruct((ROWS, OCC // NZ, TILE), f32),
        in_specs=in_vmem(1),
        out_specs=in_vmem(1)[0],
        compiler_params=pltpu.CompilerParams(vmem_limit_bytes=VMEM),
        cost_estimate=cost(1),
        name="add_up",
    )(parts)
    return jnp.swapaxes(total, 1, 2)


def solution(mesh):
    fine = Mesh(mesh.devices.reshape(NX, NY, NC, NZ), ("x", "y", "core", "z"))
    tensor = ("x", "y", "core")
    in_specs = (
        P(tensor, None, None),
        P(),
        P(tensor, "z", None, None),
        P(tensor, None),
        P(),
    )

    return jax.shard_map(
        local,
        mesh=fine,
        in_specs=in_specs,
        out_specs=P(tensor, None, "z"),
        check_vma=False,
    )
```

```python
import jax
import jax.numpy as jnp
from jax import lax
from jax.experimental import pallas as pl
from jax.experimental.pallas import tpu as pltpu
from jax.sharding import Mesh, PartitionSpec as P


NX, NY, NC, NZ = 4, 8, 2, 8
BLK = 1024
ROWS = 16
PAIRS = ROWS // 2
TILE = 64
NIRR = 8
SUB = TILE // NZ
PER_Z = 8
OCC = 128
BACKWARD = list(range(NZ))[::-1]
VMEM = 16 << 20
CONTR = NZ * PER_Z * SUB

bf16 = jnp.bfloat16
f32 = jnp.float32


def split_tiles(tiles_ref, out_ref):
    eye = (
        lax.broadcasted_iota(jnp.int32, (TILE, TILE), 0)
        == lax.broadcasted_iota(jnp.int32, (TILE, TILE), 1)
    ).astype(bf16)

    def step(pair, carry):
        for n in range(PER_Z):
            both = jnp.concatenate(
                [tiles_ref[2 * pair, n], tiles_ref[2 * pair + 1, n]], axis=0
            )
            turned = lax.dot_general(
                eye, both, (((1,), (1,)), ((), ())), preferred_element_type=f32
            ).astype(bf16)
            for z in range(NZ):
                out_ref[z, pair, n * SUB : (n + 1) * SUB, :] = turned[
                    z * SUB : (z + 1) * SUB, :
                ]
        return carry

    lax.fori_loop(0, PAIRS, step, 0)


def find(table_ref, row_irrep_ref, cols_ref, out_ref):
    def step(row, carry):
        irrep = row_irrep_ref[row]
        for n in range(NZ * PER_Z):
            entry = table_ref[cols_ref[row, n]]
            out_ref[row, n] = jnp.where(
                jnp.bitwise_and(entry, NIRR - 1) == irrep,
                lax.shift_right_logical(entry, 3),
                BLK,
            )
        return carry

    lax.fori_loop(0, ROWS, step, 0)


def pick(where_ref, *refs):
    pieces, out_ref, amp, sem = refs[:-3], *refs[-3:]
    size = BLK // len(pieces)
    copies = [
        pltpu.make_async_copy(piece, amp.at[pl.ds(k * size, size)], sem.at[k])
        for k, piece in enumerate(pieces)
    ]
    for copy in copies:
        copy.start()
    amp[BLK] = jnp.zeros((SUB, OCC), bf16)
    for copy in copies:
        copy.wait()

    def step(pair, carry):
        for parity in range(2):
            for n in range(NZ * PER_Z):
                at = where_ref[2 * pair + parity, n]
                out_ref[
                    pair, n * SUB : (n + 1) * SUB, parity * OCC : (parity + 1) * OCC
                ] = amp[at]
        return carry

    lax.fori_loop(0, PAIRS, step, 0)


def contract(picked_ref, tiles_ref, out_ref):
    low = lax.broadcasted_iota(jnp.int32, (OCC, OCC), 1) < TILE
    for pair in range(PAIRS):
        tiles = tiles_ref[:, pair].reshape(CONTR, OCC)
        both = lax.dot_general(
            picked_ref[pair], tiles, (((0,), (0,)), ((), ())), preferred_element_type=f32
        )
        total = jnp.where(low, both[:OCC], both[OCC:])
        for i, z in enumerate(BACKWARD):
            out_ref[i, pair] = total[z * (OCC // NZ) : (z + 1) * (OCC // NZ)]


def add_up(parts_ref, out_ref):
    total = parts_ref[0]
    for z in range(1, NZ):
        total = total + parts_ref[z]
    for pair in range(PAIRS):
        out_ref[2 * pair] = total[pair, :, :TILE]
        out_ref[2 * pair + 1] = total[pair, :, TILE:]


def in_vmem(n):
    return [pl.BlockSpec(memory_space=pltpu.VMEM)] * n


def cost(mib):
    return pl.CostEstimate(
        flops=1 << 28, bytes_accessed=mib << 20, transcendentals=0
    )


def local(amplitudes, block_slot, integrals, tile_cols, irreps):
    x, y = lax.axis_index("x"), lax.axis_index("y")
    core, z = lax.axis_index("core"), lax.axis_index("z")

    part = lax.dynamic_slice_in_dim(amplitudes, z * SUB, SUB, 1)
    to_y = jnp.broadcast_to(part, (NY, ROWS, SUB, OCC))
    along_y = lax.all_to_all(to_y, "y", 0, 0, tiled=False)
    along_y = along_y.reshape(NY * ROWS, SUB, OCC)
    pieces = [along_y]
    for k in (1, 2, 3):
        shift = [((i + k) % NX, i) for i in range(NX)]
        pieces.append(lax.ppermute(along_y, "x", shift))
    own = jnp.concatenate(pieces, axis=0)
    other = lax.ppermute(own, "core", [(0, 1), (1, 0)])

    split = pl.pallas_call(
        split_tiles,
        out_shape=jax.ShapeDtypeStruct((NZ, PAIRS, PER_Z * SUB, OCC), bf16),
        in_specs=in_vmem(1),
        out_specs=in_vmem(1)[0],
        compiler_params=pltpu.CompilerParams(vmem_limit_bytes=VMEM),
        cost_estimate=cost(3),
        name="split_tiles",
    )(integrals)
    tiles = lax.all_to_all(split, "z", 0, 0, tiled=False)

    holder = block_slot // ROWS
    holder_x, holder_y = holder // (NY * NC), (holder // NC) % NY
    place = ((holder_x - x) % NX) * NY + holder_y + (holder + core) % NC * (NX * NY)
    table = (place * ROWS + block_slot % ROWS) * NIRR + irreps
    first_row = ((x * NY + y) * NC + core) * ROWS
    row_irrep = lax.dynamic_slice_in_dim(irreps, first_row, ROWS, 0)
    where = pl.pallas_call(
        find,
        out_shape=jax.ShapeDtypeStruct((ROWS, NZ * PER_Z), jnp.int32),
        in_specs=[pl.BlockSpec(memory_space=pltpu.SMEM)] * 3,
        out_specs=pl.BlockSpec(memory_space=pltpu.SMEM),
        compiler_params=pltpu.CompilerParams(vmem_limit_bytes=VMEM),
        cost_estimate=cost(1),
        name="find",
    )(table, row_irrep, tile_cols)

    picked = pl.pallas_call(
        pick,
        out_shape=jax.ShapeDtypeStruct((PAIRS, CONTR, 2 * OCC), bf16),
        in_specs=[pl.BlockSpec(memory_space=pltpu.SMEM)]
        + [pl.BlockSpec(memory_space=pl.ANY)] * NC,
        out_specs=in_vmem(1)[0],
        scratch_shapes=[
            pltpu.VMEM((BLK + 8, SUB, OCC), bf16),
            pltpu.SemaphoreType.DMA((NC,)),
        ],
        compiler_params=pltpu.CompilerParams(vmem_limit_bytes=VMEM),
        cost_estimate=cost(6),
        name="pick",
    )(where, own, other)
    sums = pl.pallas_call(
        contract,
        out_shape=jax.ShapeDtypeStruct((NZ, PAIRS, OCC // NZ, OCC), f32),
        in_specs=in_vmem(2),
        out_specs=in_vmem(1)[0],
        compiler_params=pltpu.CompilerParams(vmem_limit_bytes=VMEM),
        cost_estimate=cost(4),
        name="contract",
    )(picked, tiles)
    parts = lax.all_to_all(sums, "z", 0, 0, axis_index_groups=[BACKWARD], tiled=False)

    total = pl.pallas_call(
        add_up,
        out_shape=jax.ShapeDtypeStruct((ROWS, OCC // NZ, TILE), f32),
        in_specs=in_vmem(1),
        out_specs=in_vmem(1)[0],
        compiler_params=pltpu.CompilerParams(vmem_limit_bytes=VMEM),
        cost_estimate=cost(1),
        name="add_up",
    )(parts)
    return jnp.swapaxes(total, 1, 2)


def solution(mesh):
    fine = Mesh(mesh.devices.reshape(NX, NY, NC, NZ), ("x", "y", "core", "z"))
    tensor = ("x", "y", "core")
    in_specs = (
        P(tensor, None, None),
        P(),
        P(tensor, "z", None, None),
        P(tensor, None),
        P(),
    )

    return jax.shard_map(
        local,
        mesh=fine,
        in_specs=in_specs,
        out_specs=P(tensor, None, "z"),
        check_vma=False,
    )
```

```python
import jax
import jax.numpy as jnp
from jax import lax
from jax.experimental import pallas as pl
from jax.experimental.pallas import tpu as pltpu
from jax.sharding import Mesh, PartitionSpec as P


NX, NY, NC, NZ = 4, 8, 2, 8
BLK = 1024
ROWS = 16
PAIRS = ROWS // 2
TILE = 64
NIRR = 8
SUB = TILE // NZ
PER_Z = 8
OCC = 128
BACKWARD = list(range(NZ))[::-1]
VMEM = 16 << 20
CONTR = NZ * PER_Z * SUB

bf16 = jnp.bfloat16
f32 = jnp.float32


def split_tiles(tiles_ref, out_ref):
    eye = (
        lax.broadcasted_iota(jnp.int32, (TILE, TILE), 0)
        == lax.broadcasted_iota(jnp.int32, (TILE, TILE), 1)
    ).astype(bf16)

    def step(pair, carry):
        for n in range(PER_Z):
            both = jnp.concatenate(
                [tiles_ref[2 * pair, n], tiles_ref[2 * pair + 1, n]], axis=0
            )
            turned = lax.dot_general(
                eye, both, (((1,), (1,)), ((), ())), preferred_element_type=f32
            ).astype(bf16)
            for z in range(NZ):
                out_ref[z, pair, n * SUB : (n + 1) * SUB, :] = turned[
                    z * SUB : (z + 1) * SUB, :
                ]
        return carry

    lax.fori_loop(0, PAIRS, step, 0)


def find(table_ref, row_irrep_ref, cols_ref, out_ref):
    def step(row, carry):
        irrep = row_irrep_ref[row]
        for n in range(NZ * PER_Z):
            entry = table_ref[cols_ref[row, n]]
            out_ref[row, n] = jnp.where(
                jnp.bitwise_and(entry, NIRR - 1) == irrep,
                lax.shift_right_logical(entry, 3),
                BLK,
            )
        return carry

    lax.fori_loop(0, ROWS, step, 0)


def pick(where_ref, *refs):
    pieces, out_ref, amp, sem = refs[:-3], *refs[-3:]
    size = BLK // len(pieces)
    copies = [
        pltpu.make_async_copy(piece, amp.at[pl.ds(k * size, size)], sem.at[k])
        for k, piece in enumerate(pieces)
    ]
    for copy in copies:
        copy.start()
    amp[BLK] = jnp.zeros((SUB, OCC), bf16)
    for copy in copies:
        copy.wait()

    def step(pair, carry):
        for parity in range(2):
            for n in range(NZ * PER_Z):
                at = where_ref[2 * pair + parity, n]
                out_ref[
                    pair, n * SUB : (n + 1) * SUB, parity * OCC : (parity + 1) * OCC
                ] = amp[at]
        return carry

    lax.fori_loop(0, PAIRS, step, 0)


def contract(picked_ref, tiles_ref, out_ref):
    low = lax.broadcasted_iota(jnp.int32, (OCC, OCC), 1) < TILE
    for pair in range(PAIRS):
        tiles = tiles_ref[:, pair].reshape(CONTR, OCC)
        both = lax.dot_general(
            picked_ref[pair], tiles, (((0,), (0,)), ((), ())), preferred_element_type=f32
        )
        total = jnp.where(low, both[:OCC], both[OCC:])
        for i, z in enumerate(BACKWARD):
            out_ref[i, pair] = total[z * (OCC // NZ) : (z + 1) * (OCC // NZ)]


def add_up(parts_ref, out_ref):
    total = parts_ref[0]
    for z in range(1, NZ):
        total = total + parts_ref[z]
    for pair in range(PAIRS):
        out_ref[2 * pair] = total[pair, :, :TILE]
        out_ref[2 * pair + 1] = total[pair, :, TILE:]


def in_vmem(n):
    return [pl.BlockSpec(memory_space=pltpu.VMEM)] * n


def cost(mib):
    return pl.CostEstimate(
        flops=1 << 28, bytes_accessed=mib << 20, transcendentals=0
    )


def local(amplitudes, block_slot, integrals, tile_cols, irreps):
    x, y = lax.axis_index("x"), lax.axis_index("y")
    core, z = lax.axis_index("core"), lax.axis_index("z")

    part = lax.dynamic_slice_in_dim(amplitudes, z * SUB, SUB, 1)
    to_y = jnp.broadcast_to(part, (NY // 2, ROWS, SUB, OCC))
    same = lax.all_to_all(
        to_y, "y", 0, 0, axis_index_groups=[[0, 2, 4, 6], [1, 3, 5, 7]], tiled=False
    ).reshape(NY // 2 * ROWS, SUB, OCC)
    near = lax.ppermute(same, "y", [(i, i ^ 1) for i in range(NY)])
    along_y = jnp.concatenate([same, near], axis=0)
    pieces = [along_y]
    for k in (1, 2, 3):
        shift = [((i + k) % NX, i) for i in range(NX)]
        pieces.append(lax.ppermute(along_y, "x", shift))
    owns, others = [], []
    for two in (pieces[:2], pieces[2:]):
        owns.append(jnp.concatenate(two, axis=0))
        others.append(lax.ppermute(owns[-1], "core", [(0, 1), (1, 0)]))

    split = pl.pallas_call(
        split_tiles,
        out_shape=jax.ShapeDtypeStruct((NZ, PAIRS, PER_Z * SUB, OCC), bf16),
        in_specs=in_vmem(1),
        out_specs=in_vmem(1)[0],
        compiler_params=pltpu.CompilerParams(vmem_limit_bytes=VMEM),
        cost_estimate=cost(3),
        name="split_tiles",
    )(integrals)
    tiles = lax.all_to_all(split, "z", 0, 0, tiled=False)

    holder = block_slot // ROWS
    holder_x, holder_y = holder // (NY * NC), (holder // NC) % NY
    near = (holder_y + y) % 2 * (NY // 2) + holder_y // 2
    place = ((holder_x - x) % NX) * NY + near + (holder + core) % NC * (NX * NY)
    table = (place * ROWS + block_slot % ROWS) * NIRR + irreps
    first_row = ((x * NY + y) * NC + core) * ROWS
    row_irrep = lax.dynamic_slice_in_dim(irreps, first_row, ROWS, 0)
    where = pl.pallas_call(
        find,
        out_shape=jax.ShapeDtypeStruct((ROWS, NZ * PER_Z), jnp.int32),
        in_specs=[pl.BlockSpec(memory_space=pltpu.SMEM)] * 3,
        out_specs=pl.BlockSpec(memory_space=pltpu.SMEM),
        compiler_params=pltpu.CompilerParams(vmem_limit_bytes=VMEM),
        cost_estimate=cost(1),
        name="find",
    )(table, row_irrep, tile_cols)

    picked = pl.pallas_call(
        pick,
        out_shape=jax.ShapeDtypeStruct((PAIRS, CONTR, 2 * OCC), bf16),
        in_specs=[pl.BlockSpec(memory_space=pltpu.SMEM)]
        + [pl.BlockSpec(memory_space=pl.ANY)] * (2 * NC),
        out_specs=in_vmem(1)[0],
        scratch_shapes=[
            pltpu.VMEM((BLK + 8, SUB, OCC), bf16),
            pltpu.SemaphoreType.DMA((2 * NC,)),
        ],
        compiler_params=pltpu.CompilerParams(vmem_limit_bytes=VMEM),
        cost_estimate=cost(6),
        name="pick",
    )(where, *owns, *others)
    sums = pl.pallas_call(
        contract,
        out_shape=jax.ShapeDtypeStruct((NZ, PAIRS, OCC // NZ, OCC), f32),
        in_specs=in_vmem(2),
        out_specs=in_vmem(1)[0],
        compiler_params=pltpu.CompilerParams(vmem_limit_bytes=VMEM),
        cost_estimate=cost(4),
        name="contract",
    )(picked, tiles)
    parts = lax.all_to_all(sums, "z", 0, 0, axis_index_groups=[BACKWARD], tiled=False)

    total = pl.pallas_call(
        add_up,
        out_shape=jax.ShapeDtypeStruct((ROWS, OCC // NZ, TILE), f32),
        in_specs=in_vmem(1),
        out_specs=in_vmem(1)[0],
        compiler_params=pltpu.CompilerParams(vmem_limit_bytes=VMEM),
        cost_estimate=cost(1),
        name="add_up",
    )(parts)
    return jnp.swapaxes(total, 1, 2)


def solution(mesh):
    fine = Mesh(mesh.devices.reshape(NX, NY, NC, NZ), ("x", "y", "core", "z"))
    tensor = ("x", "y", "core")
    in_specs = (
        P(tensor, None, None),
        P(),
        P(tensor, "z", None, None),
        P(tensor, None),
        P(),
    )

    return jax.shard_map(
        local,
        mesh=fine,
        in_specs=in_specs,
        out_specs=P(tensor, None, "z"),
        check_vma=False,
    )
```

```python
import jax
import jax.numpy as jnp
from jax import lax
from jax.experimental import pallas as pl
from jax.experimental.pallas import tpu as pltpu
from jax.sharding import Mesh, PartitionSpec as P


NX, NY, NC, NZ = 4, 8, 2, 8
BLK = 1024
ROWS = 16
PAIRS = ROWS // 2
TILE = 64
NIRR = 8
SUB = TILE // NZ
PER_Z = 8
OCC = 128
BACKWARD = list(range(NZ))[::-1]
STEPS = 32000.0
SMALLEST = 2.0**-100
VMEM = 16 << 20
CONTR = NZ * PER_Z * SUB

bf16 = jnp.bfloat16
f32 = jnp.float32


def split_tiles(tiles_ref, out_ref):
    eye = (
        lax.broadcasted_iota(jnp.int32, (TILE, TILE), 0)
        == lax.broadcasted_iota(jnp.int32, (TILE, TILE), 1)
    ).astype(bf16)

    def step(pair, carry):
        for n in range(PER_Z):
            both = jnp.concatenate(
                [tiles_ref[2 * pair, n], tiles_ref[2 * pair + 1, n]], axis=0
            )
            turned = lax.dot_general(
                eye, both, (((1,), (1,)), ((), ())), preferred_element_type=f32
            ).astype(bf16)
            for z in range(NZ):
                out_ref[z, pair, n * SUB : (n + 1) * SUB, :] = turned[
                    z * SUB : (z + 1) * SUB, :
                ]
        return carry

    lax.fori_loop(0, PAIRS, step, 0)


def find(table_ref, row_irrep_ref, cols_ref, out_ref):
    def step(row, carry):
        irrep = row_irrep_ref[row]
        for n in range(NZ * PER_Z):
            entry = table_ref[cols_ref[row, n]]
            out_ref[row, n] = jnp.where(
                jnp.bitwise_and(entry, NIRR - 1) == irrep,
                lax.shift_right_logical(entry, 3),
                BLK,
            )
        return carry

    lax.fori_loop(0, ROWS, step, 0)


def pick(where_ref, *refs):
    pieces, out_ref, amp, sem = refs[:-3], *refs[-3:]
    size = BLK // len(pieces)
    copies = [
        pltpu.make_async_copy(piece, amp.at[pl.ds(k * size, size)], sem.at[k])
        for k, piece in enumerate(pieces)
    ]
    for copy in copies:
        copy.start()
    amp[BLK] = jnp.zeros((SUB, OCC), bf16)
    for copy in copies:
        copy.wait()

    def step(pair, carry):
        for parity in range(2):
            for n in range(NZ * PER_Z):
                at = where_ref[2 * pair + parity, n]
                out_ref[
                    pair, n * SUB : (n + 1) * SUB, parity * OCC : (parity + 1) * OCC
                ] = amp[at]
        return carry

    lax.fori_loop(0, PAIRS, step, 0)


def contract(picked_ref, tiles_ref, out_ref, powers_ref):
    low = lax.broadcasted_iota(jnp.int32, (OCC, OCC), 1) < TILE
    powers_ref[...] = jnp.zeros_like(powers_ref)
    for pair in range(PAIRS):
        tiles = tiles_ref[:, pair].reshape(CONTR, OCC)
        both = lax.dot_general(
            picked_ref[pair], tiles, (((0,), (0,)), ((), ())), preferred_element_type=f32
        )
        total = jnp.where(low, both[:OCC], both[OCC:]).reshape(NZ, OCC // NZ, OCC)
        top = jnp.max(jnp.abs(total), axis=1)
        power = jnp.ceil(jnp.log2(jnp.maximum(top, SMALLEST)))
        scale = jnp.exp2(-power) * STEPS
        for i, z in enumerate(BACKWARD):
            fixed = jnp.round(total[z] * scale[z : z + 1])
            out_ref[i, pair] = fixed.astype(jnp.int32).astype(jnp.int16)
            powers_ref[i, pair : pair + 1, :] = power[z : z + 1]
    for i in range(NZ):
        out_ref[i, PAIRS] = powers_ref[i].astype(jnp.int32).astype(jnp.int16)


def add_up(parts_ref, out_ref):
    scales = [
        jnp.exp2(parts_ref[z, PAIRS].astype(jnp.int32).astype(f32)) * (1.0 / STEPS)
        for z in range(NZ)
    ]
    for pair in range(PAIRS):
        total = jnp.zeros((OCC // NZ, OCC), f32)
        for z in range(NZ):
            fixed = parts_ref[z, pair].astype(jnp.int32).astype(f32)
            total = total + fixed * scales[z][pair : pair + 1]
        out_ref[2 * pair] = total[:, :TILE]
        out_ref[2 * pair + 1] = total[:, TILE:]


def in_vmem(n):
    return [pl.BlockSpec(memory_space=pltpu.VMEM)] * n


def cost(mib):
    return pl.CostEstimate(
        flops=1 << 28, bytes_accessed=mib << 20, transcendentals=0
    )


def local(amplitudes, block_slot, integrals, tile_cols, irreps):
    x, y = lax.axis_index("x"), lax.axis_index("y")
    core, z = lax.axis_index("core"), lax.axis_index("z")

    part = lax.dynamic_slice_in_dim(amplitudes, z * SUB, SUB, 1)
    to_y = jnp.broadcast_to(part, (NY // 2, ROWS, SUB, OCC))
    same = lax.all_to_all(
        to_y, "y", 0, 0, axis_index_groups=[[0, 2, 4, 6], [1, 3, 5, 7]], tiled=False
    ).reshape(NY // 2 * ROWS, SUB, OCC)
    near = lax.ppermute(same, "y", [(i, i ^ 1) for i in range(NY)])
    along_y = jnp.concatenate([same, near], axis=0)
    pieces = [along_y]
    for k in (1, 2, 3):
        shift = [((i + k) % NX, i) for i in range(NX)]
        pieces.append(lax.ppermute(along_y, "x", shift))
    owns, others = [], []
    for two in (pieces[:2], pieces[2:]):
        owns.append(jnp.concatenate(two, axis=0))
        others.append(lax.ppermute(owns[-1], "core", [(0, 1), (1, 0)]))

    split = pl.pallas_call(
        split_tiles,
        out_shape=jax.ShapeDtypeStruct((NZ, PAIRS, PER_Z * SUB, OCC), bf16),
        in_specs=in_vmem(1),
        out_specs=in_vmem(1)[0],
        compiler_params=pltpu.CompilerParams(vmem_limit_bytes=VMEM),
        cost_estimate=cost(3),
        name="split_tiles",
    )(integrals)
    tiles = lax.all_to_all(split, "z", 0, 0, tiled=False)

    holder = block_slot // ROWS
    holder_x, holder_y = holder // (NY * NC), (holder // NC) % NY
    near = (holder_y + y) % 2 * (NY // 2) + holder_y // 2
    place = ((holder_x - x) % NX) * NY + near + (holder + core) % NC * (NX * NY)
    table = (place * ROWS + block_slot % ROWS) * NIRR + irreps
    first_row = ((x * NY + y) * NC + core) * ROWS
    row_irrep = lax.dynamic_slice_in_dim(irreps, first_row, ROWS, 0)
    where = pl.pallas_call(
        find,
        out_shape=jax.ShapeDtypeStruct((ROWS, NZ * PER_Z), jnp.int32),
        in_specs=[pl.BlockSpec(memory_space=pltpu.SMEM)] * 3,
        out_specs=pl.BlockSpec(memory_space=pltpu.SMEM),
        compiler_params=pltpu.CompilerParams(vmem_limit_bytes=VMEM),
        cost_estimate=cost(1),
        name="find",
    )(table, row_irrep, tile_cols)

    picked = pl.pallas_call(
        pick,
        out_shape=jax.ShapeDtypeStruct((PAIRS, CONTR, 2 * OCC), bf16),
        in_specs=[pl.BlockSpec(memory_space=pltpu.SMEM)]
        + [pl.BlockSpec(memory_space=pl.ANY)] * (2 * NC),
        out_specs=in_vmem(1)[0],
        scratch_shapes=[
            pltpu.VMEM((BLK + 8, SUB, OCC), bf16),
            pltpu.SemaphoreType.DMA((2 * NC,)),
        ],
        compiler_params=pltpu.CompilerParams(vmem_limit_bytes=VMEM),
        cost_estimate=cost(6),
        name="pick",
    )(where, *owns, *others)
    sums = pl.pallas_call(
        contract,
        out_shape=jax.ShapeDtypeStruct((NZ, PAIRS + 1, OCC // NZ, OCC), jnp.int16),
        in_specs=in_vmem(2),
        out_specs=in_vmem(1)[0],
        scratch_shapes=[pltpu.VMEM((NZ, OCC // NZ, OCC), f32)],
        compiler_params=pltpu.CompilerParams(vmem_limit_bytes=VMEM),
        cost_estimate=cost(4),
        name="contract",
    )(picked, tiles)
    parts = lax.all_to_all(sums, "z", 0, 0, axis_index_groups=[BACKWARD], tiled=False)

    total = pl.pallas_call(
        add_up,
        out_shape=jax.ShapeDtypeStruct((ROWS, OCC // NZ, TILE), f32),
        in_specs=in_vmem(1),
        out_specs=in_vmem(1)[0],
        compiler_params=pltpu.CompilerParams(vmem_limit_bytes=VMEM),
        cost_estimate=cost(1),
        name="add_up",
    )(parts)
    return jnp.swapaxes(total, 1, 2)


def solution(mesh):
    fine = Mesh(mesh.devices.reshape(NX, NY, NC, NZ), ("x", "y", "core", "z"))
    tensor = ("x", "y", "core")
    in_specs = (
        P(tensor, None, None),
        P(),
        P(tensor, "z", None, None),
        P(tensor, None),
        P(),
    )

    return jax.shard_map(
        local,
        mesh=fine,
        in_specs=in_specs,
        out_specs=P(tensor, None, "z"),
        check_vma=False,
    )
```

```python
import jax
import jax.numpy as jnp
from jax import lax
from jax.experimental import pallas as pl
from jax.experimental.pallas import tpu as pltpu
from jax.sharding import Mesh, PartitionSpec as P


NX, NY, NC, NZ = 4, 8, 2, 8
BLK = 1024
ROWS = 16
PAIRS = ROWS // 2
TILE = 64
NIRR = 8
SUB = TILE // NZ
PER_Z = 8
OCC = 128
TILES_ORDER = [0, 1, 2, 3, 4, 5, 6, 7]
SUMS_ORDER = [4, 5, 6, 7, 0, 1, 2, 3]
STEPS = 32000.0
SMALLEST = 2.0**-100
VMEM = 16 << 20
CONTR = NZ * PER_Z * SUB

bf16 = jnp.bfloat16
f32 = jnp.float32


def split_tiles(tiles_ref, out_ref):
    eye = (
        lax.broadcasted_iota(jnp.int32, (TILE, TILE), 0)
        == lax.broadcasted_iota(jnp.int32, (TILE, TILE), 1)
    ).astype(bf16)

    def step(pair, carry):
        for n in range(PER_Z):
            both = jnp.concatenate(
                [tiles_ref[2 * pair, n], tiles_ref[2 * pair + 1, n]], axis=0
            )
            turned = lax.dot_general(
                eye, both, (((1,), (1,)), ((), ())), preferred_element_type=f32
            ).astype(bf16)
            for i, z in enumerate(TILES_ORDER):
                out_ref[i, pair, n * SUB : (n + 1) * SUB, :] = turned[
                    z * SUB : (z + 1) * SUB, :
                ]
        return carry

    lax.fori_loop(0, PAIRS, step, 0)


def find(table_ref, row_irrep_ref, cols_ref, out_ref):
    def step(row, carry):
        irrep = row_irrep_ref[row]
        for n in range(NZ * PER_Z):
            entry = table_ref[
                cols_ref[row, TILES_ORDER[n // PER_Z] * PER_Z + n % PER_Z]
            ]
            out_ref[row, n] = jnp.where(
                jnp.bitwise_and(entry, NIRR - 1) == irrep,
                lax.shift_right_logical(entry, 3),
                BLK,
            )
        return carry

    lax.fori_loop(0, ROWS, step, 0)


def pick(where_ref, *refs):
    pieces, out_ref, amp, sem = refs[:-3], *refs[-3:]
    size = BLK // len(pieces)
    copies = [
        pltpu.make_async_copy(piece, amp.at[pl.ds(k * size, size)], sem.at[k])
        for k, piece in enumerate(pieces)
    ]
    for copy in copies:
        copy.start()
    amp[BLK] = jnp.zeros((SUB, OCC), bf16)
    for copy in copies:
        copy.wait()

    def step(pair, carry):
        for parity in range(2):
            for n in range(NZ * PER_Z):
                at = where_ref[2 * pair + parity, n]
                out_ref[
                    pair, n * SUB : (n + 1) * SUB, parity * OCC : (parity + 1) * OCC
                ] = amp[at]
        return carry

    lax.fori_loop(0, PAIRS, step, 0)


def contract(picked_ref, tiles_ref, out_ref, powers_ref):
    low = lax.broadcasted_iota(jnp.int32, (OCC, OCC), 1) < TILE
    powers_ref[...] = jnp.zeros_like(powers_ref)
    for pair in range(PAIRS):
        tiles = tiles_ref[:, pair].reshape(CONTR, OCC)
        both = lax.dot_general(
            picked_ref[pair], tiles, (((0,), (0,)), ((), ())), preferred_element_type=f32
        )
        total = jnp.where(low, both[:OCC], both[OCC:]).reshape(NZ, OCC // NZ, OCC)
        top = jnp.max(jnp.abs(total), axis=1)
        power = jnp.ceil(jnp.log2(jnp.maximum(top, SMALLEST)))
        scale = jnp.exp2(-power) * STEPS
        for i, z in enumerate(SUMS_ORDER):
            fixed = jnp.round(total[z] * scale[z : z + 1])
            out_ref[i, pair] = fixed.astype(jnp.int32).astype(jnp.int16)
            powers_ref[i, pair : pair + 1, :] = power[z : z + 1]
    for i in range(NZ):
        out_ref[i, PAIRS] = powers_ref[i].astype(jnp.int32).astype(jnp.int16)


def add_up(parts_ref, out_ref):
    scales = [
        jnp.exp2(parts_ref[z, PAIRS].astype(jnp.int32).astype(f32)) * (1.0 / STEPS)
        for z in range(NZ)
    ]
    for pair in range(PAIRS):
        total = jnp.zeros((OCC // NZ, OCC), f32)
        for z in range(NZ):
            fixed = parts_ref[z, pair].astype(jnp.int32).astype(f32)
            total = total + fixed * scales[z][pair : pair + 1]
        out_ref[2 * pair] = total[:, :TILE]
        out_ref[2 * pair + 1] = total[:, TILE:]


def in_vmem(n):
    return [pl.BlockSpec(memory_space=pltpu.VMEM)] * n


def cost(mib):
    return pl.CostEstimate(
        flops=1 << 28, bytes_accessed=mib << 20, transcendentals=0
    )


def local(amplitudes, block_slot, integrals, tile_cols, irreps):
    x, y = lax.axis_index("x"), lax.axis_index("y")
    core, z = lax.axis_index("core"), lax.axis_index("z")

    part = lax.dynamic_slice_in_dim(amplitudes, z * SUB, SUB, 1)
    to_y = jnp.broadcast_to(part, (NY // 2, ROWS, SUB, OCC))
    same = lax.all_to_all(
        to_y, "y", 0, 0, axis_index_groups=[[0, 2, 4, 6], [1, 3, 5, 7]], tiled=False
    ).reshape(NY // 2 * ROWS, SUB, OCC)
    near = lax.ppermute(same, "y", [(i, i ^ 1) for i in range(NY)])
    along_y = jnp.concatenate([same, near], axis=0)
    pieces = [along_y]
    for k in (1, 2, 3):
        shift = [((i + k) % NX, i) for i in range(NX)]
        pieces.append(lax.ppermute(along_y, "x", shift))
    owns, others = [], []
    for two in (pieces[:2], pieces[2:]):
        owns.append(jnp.concatenate(two, axis=0))
        others.append(lax.ppermute(owns[-1], "core", [(0, 1), (1, 0)]))

    split = pl.pallas_call(
        split_tiles,
        out_shape=jax.ShapeDtypeStruct((NZ, PAIRS, PER_Z * SUB, OCC), bf16),
        in_specs=in_vmem(1),
        out_specs=in_vmem(1)[0],
        compiler_params=pltpu.CompilerParams(vmem_limit_bytes=VMEM),
        cost_estimate=cost(3),
        name="split_tiles",
    )(integrals)
    tiles = lax.all_to_all(split, "z", 0, 0, tiled=False)

    holder = block_slot // ROWS
    holder_x, holder_y = holder // (NY * NC), (holder // NC) % NY
    near = (holder_y + y) % 2 * (NY // 2) + holder_y // 2
    place = ((holder_x - x) % NX) * NY + near + (holder + core) % NC * (NX * NY)
    table = (place * ROWS + block_slot % ROWS) * NIRR + irreps
    first_row = ((x * NY + y) * NC + core) * ROWS
    row_irrep = lax.dynamic_slice_in_dim(irreps, first_row, ROWS, 0)
    where = pl.pallas_call(
        find,
        out_shape=jax.ShapeDtypeStruct((ROWS, NZ * PER_Z), jnp.int32),
        in_specs=[pl.BlockSpec(memory_space=pltpu.SMEM)] * 3,
        out_specs=pl.BlockSpec(memory_space=pltpu.SMEM),
        compiler_params=pltpu.CompilerParams(vmem_limit_bytes=VMEM),
        cost_estimate=cost(1),
        name="find",
    )(table, row_irrep, tile_cols)

    picked = pl.pallas_call(
        pick,
        out_shape=jax.ShapeDtypeStruct((PAIRS, CONTR, 2 * OCC), bf16),
        in_specs=[pl.BlockSpec(memory_space=pltpu.SMEM)]
        + [pl.BlockSpec(memory_space=pl.ANY)] * (2 * NC),
        out_specs=in_vmem(1)[0],
        scratch_shapes=[
            pltpu.VMEM((BLK + 8, SUB, OCC), bf16),
            pltpu.SemaphoreType.DMA((2 * NC,)),
        ],
        compiler_params=pltpu.CompilerParams(vmem_limit_bytes=VMEM),
        cost_estimate=cost(6),
        name="pick",
    )(where, *owns, *others)
    sums = pl.pallas_call(
        contract,
        out_shape=jax.ShapeDtypeStruct((NZ, PAIRS + 1, OCC // NZ, OCC), jnp.int16),
        in_specs=in_vmem(2),
        out_specs=in_vmem(1)[0],
        scratch_shapes=[pltpu.VMEM((NZ, OCC // NZ, OCC), f32)],
        compiler_params=pltpu.CompilerParams(vmem_limit_bytes=VMEM),
        cost_estimate=cost(4),
        name="contract",
    )(picked, tiles)
    parts = lax.all_to_all(sums, "z", 0, 0, axis_index_groups=[SUMS_ORDER], tiled=False)

    total = pl.pallas_call(
        add_up,
        out_shape=jax.ShapeDtypeStruct((ROWS, OCC // NZ, TILE), f32),
        in_specs=in_vmem(1),
        out_specs=in_vmem(1)[0],
        compiler_params=pltpu.CompilerParams(vmem_limit_bytes=VMEM),
        cost_estimate=cost(1),
        name="add_up",
    )(parts)
    return jnp.swapaxes(total, 1, 2)


def solution(mesh):
    fine = Mesh(mesh.devices.reshape(NX, NY, NC, NZ), ("x", "y", "core", "z"))
    tensor = ("x", "y", "core")
    in_specs = (
        P(tensor, None, None),
        P(),
        P(tensor, "z", None, None),
        P(tensor, None),
        P(),
    )

    return jax.shard_map(
        local,
        mesh=fine,
        in_specs=in_specs,
        out_specs=P(tensor, None, "z"),
        check_vma=False,
    )
```

```python
import jax
import jax.numpy as jnp
from jax import lax
from jax.experimental import pallas as pl
from jax.experimental.pallas import tpu as pltpu
from jax.sharding import Mesh, PartitionSpec as P


NX, NY, NC, NZ = 4, 8, 2, 8
BLK = 1024
ROWS = 16
PAIRS = ROWS // 2
TILE = 64
NIRR = 8
SUB = TILE // NZ
PER_Z = 8
OCC = 128
TILES_ORDER = [0, 1, 2, 3, 4, 5, 6, 7]
SUMS_ORDER = [4, 5, 6, 7, 0, 1, 2, 3]
STEPS = 32000.0
SMALLEST = 2.0**-100
VMEM = 16 << 20
CONTR = NZ * PER_Z * SUB

bf16 = jnp.bfloat16
f32 = jnp.float32


def split_tiles(tiles_ref, out_ref):
    eye = (
        lax.broadcasted_iota(jnp.int32, (TILE, TILE), 0)
        == lax.broadcasted_iota(jnp.int32, (TILE, TILE), 1)
    ).astype(bf16)

    def step(pair, carry):
        for n in range(PER_Z):
            both = jnp.concatenate(
                [tiles_ref[2 * pair, n], tiles_ref[2 * pair + 1, n]], axis=0
            )
            turned = lax.dot_general(
                eye, both, (((1,), (1,)), ((), ())), preferred_element_type=f32
            ).astype(bf16)
            for i, z in enumerate(TILES_ORDER):
                out_ref[i, pair, n * SUB : (n + 1) * SUB, :] = turned[
                    z * SUB : (z + 1) * SUB, :
                ]
        return carry

    lax.fori_loop(0, PAIRS, step, 0)


def find(table_ref, row_irrep_ref, cols_ref, out_ref):
    def step(row, carry):
        irrep = row_irrep_ref[row]
        for n in range(NZ * PER_Z):
            entry = table_ref[
                cols_ref[row, TILES_ORDER[n // PER_Z] * PER_Z + n % PER_Z]
            ]
            out_ref[row, n] = jnp.where(
                jnp.bitwise_and(entry, NIRR - 1) == irrep,
                lax.shift_right_logical(entry, 3),
                BLK,
            )
        return carry

    lax.fori_loop(0, ROWS, step, 0)


def pick(where_ref, *refs):
    pieces, out_ref, amp, sem = refs[:-3], *refs[-3:]
    size = BLK // len(pieces)
    copies = [
        pltpu.make_async_copy(piece, amp.at[pl.ds(k * size, size)], sem.at[k])
        for k, piece in enumerate(pieces)
    ]
    for copy in copies:
        copy.start()
    amp[BLK] = jnp.zeros((SUB, OCC), bf16)
    for copy in copies:
        copy.wait()

    def step(pair, carry):
        for parity in range(2):
            for n in range(NZ * PER_Z):
                at = where_ref[2 * pair + parity, n]
                out_ref[
                    pair, n * SUB : (n + 1) * SUB, parity * OCC : (parity + 1) * OCC
                ] = amp[at]
        return carry

    lax.fori_loop(0, PAIRS, step, 0)


def contract(picked_ref, tiles_ref, out_ref, powers_ref):
    low = lax.broadcasted_iota(jnp.int32, (OCC, OCC), 1) < TILE
    powers_ref[...] = jnp.zeros_like(powers_ref)
    for pair in range(PAIRS):
        tiles = tiles_ref[:, pair].reshape(CONTR, OCC)
        both = lax.dot_general(
            picked_ref[pair], tiles, (((0,), (0,)), ((), ())), preferred_element_type=f32
        )
        total = jnp.where(low, both[:OCC], both[OCC:]).reshape(NZ, OCC // NZ, OCC)
        top = jnp.max(jnp.abs(total), axis=1)
        power = jnp.ceil(jnp.log2(jnp.maximum(top, SMALLEST)))
        scale = jnp.exp2(-power) * STEPS
        for i, z in enumerate(SUMS_ORDER):
            fixed = jnp.round(total[z] * scale[z : z + 1])
            out_ref[i, pair] = fixed.astype(jnp.int32).astype(jnp.int16)
            powers_ref[i, pair : pair + 1, :] = power[z : z + 1]
    for i in range(NZ):
        out_ref[i, PAIRS] = powers_ref[i].astype(jnp.int32).astype(jnp.int16)


def add_up(parts_ref, out_ref):
    scales = [
        jnp.exp2(parts_ref[z, PAIRS].astype(jnp.int32).astype(f32)) * (1.0 / STEPS)
        for z in range(NZ)
    ]
    for pair in range(PAIRS):
        total = jnp.zeros((OCC // NZ, OCC), f32)
        for z in range(NZ):
            fixed = parts_ref[z, pair].astype(jnp.int32).astype(f32)
            total = total + fixed * scales[z][pair : pair + 1]
        out_ref[2 * pair] = total[:, :TILE]
        out_ref[2 * pair + 1] = total[:, TILE:]


def in_vmem(n):
    return [pl.BlockSpec(memory_space=pltpu.VMEM)] * n


def cost(mib):
    return pl.CostEstimate(
        flops=1 << 28, bytes_accessed=mib << 20, transcendentals=0
    )


def local(amplitudes, block_slot, integrals, tile_cols, irreps):
    x, y = lax.axis_index("x"), lax.axis_index("y")
    core, z = lax.axis_index("core"), lax.axis_index("z")

    part = lax.dynamic_slice_in_dim(amplitudes, z * SUB, SUB, 1)
    to_y = jnp.broadcast_to(part, (NY // 2, ROWS, SUB, OCC))
    same = lax.all_to_all(
        to_y, "y", 0, 0, axis_index_groups=[[0, 2, 4, 6], [1, 3, 5, 7]], tiled=False
    ).reshape(NY // 2 * ROWS, SUB, OCC)
    near = lax.ppermute(same, "y", [(i, i ^ 1) for i in range(NY)])
    along_y = jnp.concatenate([same, near], axis=0)
    pieces = [along_y]
    for k in (1, 2, 3):
        shift = [((i + k) % NX, i) for i in range(NX)]
        pieces.append(lax.ppermute(along_y, "x", shift))
    owns, others = [], []
    for two in (pieces[::2], pieces[1::2]):
        owns.append(jnp.concatenate(two, axis=0))
        others.append(lax.ppermute(owns[-1], "core", [(0, 1), (1, 0)]))

    split = pl.pallas_call(
        split_tiles,
        out_shape=jax.ShapeDtypeStruct((NZ, PAIRS, PER_Z * SUB, OCC), bf16),
        in_specs=in_vmem(1),
        out_specs=in_vmem(1)[0],
        compiler_params=pltpu.CompilerParams(vmem_limit_bytes=VMEM),
        cost_estimate=cost(3),
        name="split_tiles",
    )(integrals)
    tiles = lax.all_to_all(split, "z", 0, 0, tiled=False)

    holder = block_slot // ROWS
    holder_x, holder_y = holder // (NY * NC), (holder // NC) % NY
    near = (holder_y + y) % 2 * (NY // 2) + holder_y // 2
    apart = (holder_x - x) % NX
    place = (apart % 2 * 2 + apart // 2) * NY + near + (holder + core) % NC * (NX * NY)
    table = (place * ROWS + block_slot % ROWS) * NIRR + irreps
    first_row = ((x * NY + y) * NC + core) * ROWS
    row_irrep = lax.dynamic_slice_in_dim(irreps, first_row, ROWS, 0)
    where = pl.pallas_call(
        find,
        out_shape=jax.ShapeDtypeStruct((ROWS, NZ * PER_Z), jnp.int32),
        in_specs=[pl.BlockSpec(memory_space=pltpu.SMEM)] * 3,
        out_specs=pl.BlockSpec(memory_space=pltpu.SMEM),
        compiler_params=pltpu.CompilerParams(vmem_limit_bytes=VMEM),
        cost_estimate=cost(1),
        name="find",
    )(table, row_irrep, tile_cols)

    picked = pl.pallas_call(
        pick,
        out_shape=jax.ShapeDtypeStruct((PAIRS, CONTR, 2 * OCC), bf16),
        in_specs=[pl.BlockSpec(memory_space=pltpu.SMEM)]
        + [pl.BlockSpec(memory_space=pl.ANY)] * (2 * NC),
        out_specs=in_vmem(1)[0],
        scratch_shapes=[
            pltpu.VMEM((BLK + 8, SUB, OCC), bf16),
            pltpu.SemaphoreType.DMA((2 * NC,)),
        ],
        compiler_params=pltpu.CompilerParams(vmem_limit_bytes=VMEM),
        cost_estimate=cost(6),
        name="pick",
    )(where, *owns, *others)
    sums = pl.pallas_call(
        contract,
        out_shape=jax.ShapeDtypeStruct((NZ, PAIRS + 1, OCC // NZ, OCC), jnp.int16),
        in_specs=in_vmem(2),
        out_specs=in_vmem(1)[0],
        scratch_shapes=[pltpu.VMEM((NZ, OCC // NZ, OCC), f32)],
        compiler_params=pltpu.CompilerParams(vmem_limit_bytes=VMEM),
        cost_estimate=cost(4),
        name="contract",
    )(picked, tiles)
    parts = lax.all_to_all(sums, "z", 0, 0, axis_index_groups=[SUMS_ORDER], tiled=False)

    total = pl.pallas_call(
        add_up,
        out_shape=jax.ShapeDtypeStruct((ROWS, OCC // NZ, TILE), f32),
        in_specs=in_vmem(1),
        out_specs=in_vmem(1)[0],
        compiler_params=pltpu.CompilerParams(vmem_limit_bytes=VMEM),
        cost_estimate=cost(1),
        name="add_up",
    )(parts)
    return jnp.swapaxes(total, 1, 2)


def solution(mesh):
    fine = Mesh(mesh.devices.reshape(NX, NY, NC, NZ), ("x", "y", "core", "z"))
    tensor = ("x", "y", "core")
    in_specs = (
        P(tensor, None, None),
        P(),
        P(tensor, "z", None, None),
        P(tensor, None),
        P(),
    )

    return jax.shard_map(
        local,
        mesh=fine,
        in_specs=in_specs,
        out_specs=P(tensor, None, "z"),
        check_vma=False,
    )
```

```python
import jax
import jax.numpy as jnp
from jax import lax
from jax.experimental import pallas as pl
from jax.experimental.pallas import tpu as pltpu
from jax.sharding import Mesh, PartitionSpec as P


NX, NY, NC, NZ = 4, 8, 2, 8
BLK = 1024
ROWS = 16
PAIRS = ROWS // 2
TILE = 64
NIRR = 8
SUB = TILE // NZ
PER_Z = 8
OCC = 128
TILES_ORDER = [7, 1, 2, 3, 4, 5, 6, 0]
SUMS_ORDER = [4, 5, 6, 7, 0, 1, 2, 3]
STEPS = 32000.0
SMALLEST = 2.0**-100
VMEM = 16 << 20
CONTR = NZ * PER_Z * SUB

bf16 = jnp.bfloat16
f32 = jnp.float32


def split_tiles(tiles_ref, out_ref):
    eye = (
        lax.broadcasted_iota(jnp.int32, (TILE, TILE), 0)
        == lax.broadcasted_iota(jnp.int32, (TILE, TILE), 1)
    ).astype(bf16)

    def step(pair, carry):
        for n in range(PER_Z):
            both = jnp.concatenate(
                [tiles_ref[2 * pair, n], tiles_ref[2 * pair + 1, n]], axis=0
            )
            turned = lax.dot_general(
                eye, both, (((1,), (1,)), ((), ())), preferred_element_type=f32
            ).astype(bf16)
            for i, z in enumerate(TILES_ORDER):
                out_ref[i, pair, n * SUB : (n + 1) * SUB, :] = turned[
                    z * SUB : (z + 1) * SUB, :
                ]
        return carry

    lax.fori_loop(0, PAIRS, step, 0)


def find(table_ref, row_irrep_ref, cols_ref, out_ref):
    def step(row, carry):
        irrep = row_irrep_ref[row]
        for n in range(NZ * PER_Z):
            entry = table_ref[
                cols_ref[row, TILES_ORDER[n // PER_Z] * PER_Z + n % PER_Z]
            ]
            out_ref[row, n] = jnp.where(
                jnp.bitwise_and(entry, NIRR - 1) == irrep,
                lax.shift_right_logical(entry, 3),
                BLK,
            )
        return carry

    lax.fori_loop(0, ROWS, step, 0)


def pick(where_ref, *refs):
    pieces, out_ref, amp, sem = refs[:-3], *refs[-3:]
    size = BLK // len(pieces)
    copies = [
        pltpu.make_async_copy(piece, amp.at[pl.ds(k * size, size)], sem.at[k])
        for k, piece in enumerate(pieces)
    ]
    for copy in copies:
        copy.start()
    amp[BLK] = jnp.zeros((SUB, OCC), bf16)
    for copy in copies:
        copy.wait()

    def step(pair, carry):
        for parity in range(2):
            for n in range(NZ * PER_Z):
                at = where_ref[2 * pair + parity, n]
                out_ref[
                    pair, n * SUB : (n + 1) * SUB, parity * OCC : (parity + 1) * OCC
                ] = amp[at]
        return carry

    lax.fori_loop(0, PAIRS, step, 0)


def contract(picked_ref, tiles_ref, out_ref, powers_ref):
    low = lax.broadcasted_iota(jnp.int32, (OCC, OCC), 1) < TILE
    powers_ref[...] = jnp.zeros_like(powers_ref)
    for pair in range(PAIRS):
        tiles = tiles_ref[:, pair].reshape(CONTR, OCC)
        both = lax.dot_general(
            picked_ref[pair], tiles, (((0,), (0,)), ((), ())), preferred_element_type=f32
        )
        total = jnp.where(low, both[:OCC], both[OCC:]).reshape(NZ, OCC // NZ, OCC)
        top = jnp.max(jnp.abs(total), axis=1)
        power = jnp.ceil(jnp.log2(jnp.maximum(top, SMALLEST)))
        scale = jnp.exp2(-power) * STEPS
        for i, z in enumerate(SUMS_ORDER):
            fixed = jnp.round(total[z] * scale[z : z + 1])
            out_ref[i, pair] = fixed.astype(jnp.int32).astype(jnp.int16)
            powers_ref[i, pair : pair + 1, :] = power[z : z + 1]
    for i in range(NZ):
        out_ref[i, PAIRS] = powers_ref[i].astype(jnp.int32).astype(jnp.int16)


def add_up(parts_ref, out_ref):
    scales = [
        jnp.exp2(parts_ref[z, PAIRS].astype(jnp.int32).astype(f32)) * (1.0 / STEPS)
        for z in range(NZ)
    ]
    for pair in range(PAIRS):
        total = jnp.zeros((OCC // NZ, OCC), f32)
        for z in range(NZ):
            fixed = parts_ref[z, pair].astype(jnp.int32).astype(f32)
            total = total + fixed * scales[z][pair : pair + 1]
        out_ref[2 * pair] = total[:, :TILE]
        out_ref[2 * pair + 1] = total[:, TILE:]


def in_vmem(n):
    return [pl.BlockSpec(memory_space=pltpu.VMEM)] * n


def cost(mib):
    return pl.CostEstimate(
        flops=1 << 28, bytes_accessed=mib << 20, transcendentals=0
    )


def local(amplitudes, block_slot, integrals, tile_cols, irreps):
    x, y = lax.axis_index("x"), lax.axis_index("y")
    core, z = lax.axis_index("core"), lax.axis_index("z")

    part = lax.dynamic_slice_in_dim(amplitudes, z * SUB, SUB, 1)
    to_y = jnp.broadcast_to(part, (NY // 2, ROWS, SUB, OCC))
    same = lax.all_to_all(
        to_y, "y", 0, 0, axis_index_groups=[[0, 2, 4, 6], [1, 3, 5, 7]], tiled=False
    ).reshape(NY // 2 * ROWS, SUB, OCC)
    near = lax.ppermute(same, "y", [(i, i ^ 1) for i in range(NY)])
    along_y = jnp.concatenate([same, near], axis=0)
    pieces = [along_y]
    for k in (1, 2, 3):
        shift = [((i + k) % NX, i) for i in range(NX)]
        pieces.append(lax.ppermute(along_y, "x", shift))
    owns, others = [], []
    for two in (pieces[::2], pieces[1::2]):
        owns.append(jnp.concatenate(two, axis=0))
        others.append(lax.ppermute(owns[-1], "core", [(0, 1), (1, 0)]))

    split = pl.pallas_call(
        split_tiles,
        out_shape=jax.ShapeDtypeStruct((NZ, PAIRS, PER_Z * SUB, OCC), bf16),
        in_specs=in_vmem(1),
        out_specs=in_vmem(1)[0],
        compiler_params=pltpu.CompilerParams(vmem_limit_bytes=VMEM),
        cost_estimate=cost(3),
        name="split_tiles",
    )(integrals)
    tiles = lax.all_to_all(
        split, "z", 0, 0, axis_index_groups=[TILES_ORDER], tiled=False
    )

    holder = block_slot // ROWS
    holder_x, holder_y = holder // (NY * NC), (holder // NC) % NY
    near = (holder_y + y) % 2 * (NY // 2) + holder_y // 2
    apart = (holder_x - x) % NX
    place = (apart % 2 * 2 + apart // 2) * NY + near + (holder + core) % NC * (NX * NY)
    table = (place * ROWS + block_slot % ROWS) * NIRR + irreps
    first_row = ((x * NY + y) * NC + core) * ROWS
    row_irrep = lax.dynamic_slice_in_dim(irreps, first_row, ROWS, 0)
    where = pl.pallas_call(
        find,
        out_shape=jax.ShapeDtypeStruct((ROWS, NZ * PER_Z), jnp.int32),
        in_specs=[pl.BlockSpec(memory_space=pltpu.SMEM)] * 3,
        out_specs=pl.BlockSpec(memory_space=pltpu.SMEM),
        compiler_params=pltpu.CompilerParams(vmem_limit_bytes=VMEM),
        cost_estimate=cost(1),
        name="find",
    )(table, row_irrep, tile_cols)

    picked = pl.pallas_call(
        pick,
        out_shape=jax.ShapeDtypeStruct((PAIRS, CONTR, 2 * OCC), bf16),
        in_specs=[pl.BlockSpec(memory_space=pltpu.SMEM)]
        + [pl.BlockSpec(memory_space=pl.ANY)] * (2 * NC),
        out_specs=in_vmem(1)[0],
        scratch_shapes=[
            pltpu.VMEM((BLK + 8, SUB, OCC), bf16),
            pltpu.SemaphoreType.DMA((2 * NC,)),
        ],
        compiler_params=pltpu.CompilerParams(vmem_limit_bytes=VMEM),
        cost_estimate=cost(6),
        name="pick",
    )(where, *owns, *others)
    sums = pl.pallas_call(
        contract,
        out_shape=jax.ShapeDtypeStruct((NZ, PAIRS + 1, OCC // NZ, OCC), jnp.int16),
        in_specs=in_vmem(2),
        out_specs=in_vmem(1)[0],
        scratch_shapes=[pltpu.VMEM((NZ, OCC // NZ, OCC), f32)],
        compiler_params=pltpu.CompilerParams(vmem_limit_bytes=VMEM),
        cost_estimate=cost(4),
        name="contract",
    )(picked, tiles)
    parts = lax.all_to_all(sums, "z", 0, 0, axis_index_groups=[SUMS_ORDER], tiled=False)

    total = pl.pallas_call(
        add_up,
        out_shape=jax.ShapeDtypeStruct((ROWS, OCC // NZ, TILE), f32),
        in_specs=in_vmem(1),
        out_specs=in_vmem(1)[0],
        compiler_params=pltpu.CompilerParams(vmem_limit_bytes=VMEM),
        cost_estimate=cost(1),
        name="add_up",
    )(parts)
    return jnp.swapaxes(total, 1, 2)


def solution(mesh):
    fine = Mesh(mesh.devices.reshape(NX, NY, NC, NZ), ("x", "y", "core", "z"))
    tensor = ("x", "y", "core")
    in_specs = (
        P(tensor, None, None),
        P(),
        P(tensor, "z", None, None),
        P(tensor, None),
        P(),
    )

    return jax.shard_map(
        local,
        mesh=fine,
        in_specs=in_specs,
        out_specs=P(tensor, None, "z"),
        check_vma=False,
    )
```

```python
import jax
import jax.numpy as jnp
from jax import lax
from jax.experimental import pallas as pl
from jax.experimental.pallas import tpu as pltpu
from jax.sharding import Mesh, PartitionSpec as P


NX, NY, NC, NZ = 4, 8, 2, 8
BLK = 1024
ROWS = 16
PAIRS = ROWS // 2
TILE = 64
NIRR = 8
SUB = TILE // NZ
PER_Z = 8
OCC = 128
TILES_ORDER = [0, 1, 2, 3, 4, 5, 6, 7]
SUMS_ORDER = [4, 5, 6, 7, 0, 1, 2, 3]
STEPS = 32000.0
SMALLEST = 2.0**-100
VMEM = 16 << 20
CONTR = NZ * PER_Z * SUB

bf16 = jnp.bfloat16
f32 = jnp.float32


def split_tiles(tiles_ref, out_ref):
    eye = (
        lax.broadcasted_iota(jnp.int32, (TILE, TILE), 0)
        == lax.broadcasted_iota(jnp.int32, (TILE, TILE), 1)
    ).astype(bf16)

    def step(pair, carry):
        for n in range(PER_Z):
            both = jnp.concatenate(
                [tiles_ref[2 * pair, n], tiles_ref[2 * pair + 1, n]], axis=0
            )
            turned = lax.dot_general(
                eye, both, (((1,), (1,)), ((), ())), preferred_element_type=f32
            ).astype(bf16)
            for i, z in enumerate(TILES_ORDER):
                out_ref[i, pair, n * SUB : (n + 1) * SUB, :] = turned[
                    z * SUB : (z + 1) * SUB, :
                ]
        return carry

    lax.fori_loop(0, PAIRS, step, 0)


def find(table_ref, row_irrep_ref, cols_ref, raw_ref, out_ref):
    def step(row, carry):
        irrep = row_irrep_ref[row]
        for n in range(NZ * PER_Z):
            entry = table_ref[
                cols_ref[row, TILES_ORDER[n // PER_Z] * PER_Z + n % PER_Z]
            ]
            out_ref[row, n] = jnp.where(
                jnp.bitwise_and(entry, NIRR - 1) == irrep,
                lax.shift_right_logical(entry, 3),
                BLK,
            )
        return carry

    lax.fori_loop(0, ROWS, step, 0)


def pick(where_ref, *refs):
    pieces, out_ref, amp, sem = refs[:-3], *refs[-3:]
    size = BLK // len(pieces)
    copies = [
        pltpu.make_async_copy(piece, amp.at[pl.ds(k * size, size)], sem.at[k])
        for k, piece in enumerate(pieces)
    ]
    for copy in copies:
        copy.start()
    amp[BLK] = jnp.zeros((SUB, OCC), bf16)
    for copy in copies:
        copy.wait()

    def step(pair, carry):
        for parity in range(2):
            for n in range(NZ * PER_Z):
                at = where_ref[2 * pair + parity, n]
                out_ref[
                    pair, n * SUB : (n + 1) * SUB, parity * OCC : (parity + 1) * OCC
                ] = amp[at]
        return carry

    lax.fori_loop(0, PAIRS, step, 0)


def contract(picked_ref, tiles_ref, out_ref, powers_ref):
    low = lax.broadcasted_iota(jnp.int32, (OCC, OCC), 1) < TILE
    powers_ref[...] = jnp.zeros_like(powers_ref)
    for pair in range(PAIRS):
        tiles = tiles_ref[:, pair].reshape(CONTR, OCC)
        both = lax.dot_general(
            picked_ref[pair], tiles, (((0,), (0,)), ((), ())), preferred_element_type=f32
        )
        total = jnp.where(low, both[:OCC], both[OCC:]).reshape(NZ, OCC // NZ, OCC)
        top = jnp.max(jnp.abs(total), axis=1)
        power = jnp.ceil(jnp.log2(jnp.maximum(top, SMALLEST)))
        scale = jnp.exp2(-power) * STEPS
        for i, z in enumerate(SUMS_ORDER):
            fixed = jnp.round(total[z] * scale[z : z + 1])
            out_ref[i, pair] = fixed.astype(jnp.int32).astype(jnp.int16)
            powers_ref[i, pair : pair + 1, :] = power[z : z + 1]
    for i in range(NZ):
        out_ref[i, PAIRS] = powers_ref[i].astype(jnp.int32).astype(jnp.int16)


def add_up(parts_ref, out_ref):
    scales = [
        jnp.exp2(parts_ref[z, PAIRS].astype(jnp.int32).astype(f32)) * (1.0 / STEPS)
        for z in range(NZ)
    ]
    for pair in range(PAIRS):
        total = jnp.zeros((OCC // NZ, OCC), f32)
        for z in range(NZ):
            fixed = parts_ref[z, pair].astype(jnp.int32).astype(f32)
            total = total + fixed * scales[z][pair : pair + 1]
        out_ref[2 * pair] = total[:, :TILE]
        out_ref[2 * pair + 1] = total[:, TILE:]


def in_vmem(n):
    return [pl.BlockSpec(memory_space=pltpu.VMEM)] * n


def cost(mib):
    return pl.CostEstimate(
        flops=1 << 28, bytes_accessed=mib << 20, transcendentals=0
    )


def local(amplitudes, block_slot, integrals, tile_cols, irreps):
    x, y = lax.axis_index("x"), lax.axis_index("y")
    core, z = lax.axis_index("core"), lax.axis_index("z")

    part = lax.dynamic_slice_in_dim(amplitudes, z * SUB, SUB, 1)
    to_y = jnp.broadcast_to(part, (NY // 2, ROWS, SUB, OCC))
    same = lax.all_to_all(
        to_y, "y", 0, 0, axis_index_groups=[[0, 2, 4, 6], [1, 3, 5, 7]], tiled=False
    ).reshape(NY // 2 * ROWS, SUB, OCC)
    near = lax.ppermute(same, "y", [(i, i ^ 1) for i in range(NY)])
    along_y = jnp.concatenate([same, near], axis=0)
    pieces = [along_y]
    for k in (1, 2, 3):
        shift = [((i + k) % NX, i) for i in range(NX)]
        pieces.append(lax.ppermute(along_y, "x", shift))
    owns, others = [], []
    for two in (pieces[:2], pieces[2:]):
        owns.append(jnp.concatenate(two, axis=0))
        others.append(lax.ppermute(owns[-1], "core", [(0, 1), (1, 0)]))

    split = pl.pallas_call(
        split_tiles,
        out_shape=jax.ShapeDtypeStruct((NZ, PAIRS, PER_Z * SUB, OCC), bf16),
        in_specs=in_vmem(1),
        out_specs=in_vmem(1)[0],
        compiler_params=pltpu.CompilerParams(vmem_limit_bytes=VMEM),
        cost_estimate=cost(3),
        name="split_tiles",
    )(integrals)
    tiles = lax.all_to_all(split, "z", 0, 0, tiled=False)

    holder = block_slot // ROWS
    holder_x, holder_y = holder // (NY * NC), (holder // NC) % NY
    near = (holder_y + y) % 2 * (NY // 2) + holder_y // 2
    place = ((holder_x - x) % NX) * NY + near + (holder + core) % NC * (NX * NY)
    table = (place * ROWS + block_slot % ROWS) * NIRR + irreps
    first_row = ((x * NY + y) * NC + core) * ROWS
    row_irrep = lax.dynamic_slice_in_dim(irreps, first_row, ROWS, 0)
    where = pl.pallas_call(
        find,
        out_shape=jax.ShapeDtypeStruct((ROWS, NZ * PER_Z), jnp.int32),
        in_specs=[pl.BlockSpec(memory_space=pltpu.SMEM)] * 3
        + [pl.BlockSpec(memory_space=pl.ANY)],
        out_specs=pl.BlockSpec(memory_space=pltpu.SMEM),
        compiler_params=pltpu.CompilerParams(vmem_limit_bytes=VMEM),
        cost_estimate=cost(1),
        name="find",
    )(table, row_irrep, tile_cols, amplitudes)

    picked = pl.pallas_call(
        pick,
        out_shape=jax.ShapeDtypeStruct((PAIRS, CONTR, 2 * OCC), bf16),
        in_specs=[pl.BlockSpec(memory_space=pltpu.SMEM)]
        + [pl.BlockSpec(memory_space=pl.ANY)] * (2 * NC),
        out_specs=in_vmem(1)[0],
        scratch_shapes=[
            pltpu.VMEM((BLK + 8, SUB, OCC), bf16),
            pltpu.SemaphoreType.DMA((2 * NC,)),
        ],
        compiler_params=pltpu.CompilerParams(vmem_limit_bytes=VMEM),
        cost_estimate=cost(6),
        name="pick",
    )(where, *owns, *others)
    sums = pl.pallas_call(
        contract,
        out_shape=jax.ShapeDtypeStruct((NZ, PAIRS + 1, OCC // NZ, OCC), jnp.int16),
        in_specs=in_vmem(2),
        out_specs=in_vmem(1)[0],
        scratch_shapes=[pltpu.VMEM((NZ, OCC // NZ, OCC), f32)],
        compiler_params=pltpu.CompilerParams(vmem_limit_bytes=VMEM),
        cost_estimate=cost(4),
        name="contract",
    )(picked, tiles)
    parts = lax.all_to_all(sums, "z", 0, 0, axis_index_groups=[SUMS_ORDER], tiled=False)

    total = pl.pallas_call(
        add_up,
        out_shape=jax.ShapeDtypeStruct((ROWS, OCC // NZ, TILE), f32),
        in_specs=in_vmem(1),
        out_specs=in_vmem(1)[0],
        compiler_params=pltpu.CompilerParams(vmem_limit_bytes=VMEM),
        cost_estimate=cost(1),
        name="add_up",
    )(parts)
    return jnp.swapaxes(total, 1, 2)


def solution(mesh):
    fine = Mesh(mesh.devices.reshape(NX, NY, NC, NZ), ("x", "y", "core", "z"))
    tensor = ("x", "y", "core")
    in_specs = (
        P(tensor, None, None),
        P(),
        P(tensor, "z", None, None),
        P(tensor, None),
        P(),
    )

    return jax.shard_map(
        local,
        mesh=fine,
        in_specs=in_specs,
        out_specs=P(tensor, None, "z"),
        check_vma=False,
    )
```
